32 devices in a mesh: img: 4 (over y, x), proto: 8 (over z, core).
Axes of the slice: x: 2, y: 2, z: 4, core: 2. Of those that a mesh axis runs over, the one named last changes fastest.
Arguments:
- student_patch_tokens: bfloat16 [4, 256, 4096], P('img', None, 'proto'), may hold values from -6 to 6
- teacher_patch_tokens: bfloat16 [4, 256, 4096], P('img', None, 'proto'), may hold values from -6 to 6
- mask_counts: int32 [4], P('img'), may hold values from 32 to 128, as said below
- mask_index: int32 [4, 128], P('img'), may hold values from 0 to 255, as said below
- student_bottleneck: bfloat16 [4096, 256], P('proto'), may hold values from -0.09375 to 0.09375
- teacher_bottleneck: bfloat16 [4096, 256], P('proto'), may hold values from -0.09375 to 0.09375
- student_protos: bfloat16 [256, 98304], P(None, 'proto'), may hold values from -60 to 60
- teacher_protos: bfloat16 [256, 98304], P(None, 'proto'), may hold values from -60 to 60
- center: float32 [98304], P('proto'), may hold values from -0.75 to 0.75
Outputs:
- image_loss: float32 [4], P('img')
- grad_protos: float32 [256, 98304], P('img', 'proto')
- grad_bottleneck: float32 [4096, 256], P('proto', 'img')
The draws below stay inside these ranges and needn't reach their ends.
Inputs may be any that keep to these rules, and one draw needn't show every extreme that they name: `mask_counts`: some image has exactly 128 masked patches. `mask_index`: the 128 entries of an image are distinct patch numbers; only the first mask_counts of them are used.
All inputs are finite; a program needn't handle non-finite values.
Results may differ from the reference program's by a relative error of at most 0.0071.
Values may be sent and summed in bfloat16 or wider, within the bound.
No kernel may reach another device: no remote copies, remote signals or barrier semaphores. Data moves between devices by JAX's collectives and lax.ppermute only.
A program may use at most 64 MiB of HBM per device.

```python
import math
import jax
import jax.numpy as jnp
from jax import lax

D = 4096
BOT = 256
PROTOS = 98304
PATCHES = 256
MASK_MAX = 128
IMAGES = 4


def draw_mask_counts(key, part):
    counts = jax.random.randint(key, (IMAGES,), MASK_MAX // 4, MASK_MAX + 1)
    chosen = jax.random.randint(jax.random.fold_in(key, 1), (), 0, IMAGES)
    counts = jnp.where(jnp.arange(IMAGES) == chosen, MASK_MAX, counts)
    return counts.astype(jnp.int32)


def draw_mask_index(key, part):
    keys = jax.random.split(jax.random.fold_in(key, 2), IMAGES)
    orders = jax.vmap(lambda single: jax.random.permutation(single, PATCHES))(keys)
    return orders[:, :MASK_MAX].astype(jnp.int32)


def proto_table(key):
    base = jax.random.normal(key, (BOT, PROTOS), jnp.float32) / math.sqrt(BOT)
    return jnp.clip(base, -60.0, 60.0)


def draw_student_protos(key, part):
    return proto_table(jax.random.fold_in(key, 11)).astype(jnp.bfloat16)


def draw_teacher_protos(key, part):
    return proto_table(jax.random.fold_in(key, 12)).astype(jnp.bfloat16)


def shard_levels(own_key, shape, pieces, least, high):
    def one(axis_at, parts):
        heights = jax.random.uniform(jax.random.fold_in(jax.random.fold_in(own_key, 6), axis_at), (parts,), jnp.float32, least / len(pieces), high / len(pieces))
        return jnp.repeat(jnp.exp(heights), shape[axis_at] // parts).reshape((-1,) + (1,) * (len(shape) - axis_at - 1))

    level = one(*pieces[0])
    for cut in pieces[1:]:
        level = level * one(*cut)
    return level


def gaussian(key, dims, width, limit, shards=(), kind=jnp.bfloat16):
    factor_of = shard_levels(key, dims, shards, -0.22, 0.18) if shards else 1.0
    entries = jax.random.normal(key, dims, jnp.float32) * width * factor_of
    return jnp.minimum(jnp.maximum(entries, -limit), limit).astype(kind)


def setup_inputs(seed: int = 0) -> dict:
    key_list = jax.random.split(jax.random.key(seed), 10)
    return {
        "student_patch_tokens": gaussian(key_list[0], (IMAGES, PATCHES, D), 1.0, 6.0, ((0, 4), (2, 8))),
        "teacher_patch_tokens": gaussian(key_list[1], (IMAGES, PATCHES, D), 1.0, 6.0, ((0, 4), (2, 8))),
        "mask_counts": draw_mask_counts(jax.random.fold_in(key_list[9], 71), 0),
        "mask_index": draw_mask_index(jax.random.fold_in(key_list[9], 71), 0),
        "student_bottleneck": gaussian(key_list[4], (D, BOT), D ** -0.5, 0.09375, ((0, 8),)),
        "teacher_bottleneck": gaussian(key_list[5], (D, BOT), D ** -0.5, 0.09375, ((0, 8),)),
        "student_protos": draw_student_protos(jax.random.fold_in(key_list[9], 71), 0),
        "teacher_protos": draw_teacher_protos(jax.random.fold_in(key_list[9], 71), 0),
        "center": gaussian(key_list[8], (PROTOS,), 0.05, 0.75, ((0, 8),), jnp.float32),
    }


EPSILON = 1e-06
STUDENT_TEMP = 0.1
TEACHER_TEMP = 0.04
LOSS_SCALE = 4096.0

def scores(units_student, units_teacher, weight, student_protos, teacher_protos, center):
    logits_student = jnp.dot(units_student, student_protos, preferred_element_type=jnp.float32) / STUDENT_TEMP
    logits_teacher = (jnp.dot(units_teacher, teacher_protos, preferred_element_type=jnp.float32) - center[None, :]) / TEACHER_TEMP
    top_student = lax.optimization_barrier(jnp.max(logits_student, axis=1))
    top_teacher = lax.optimization_barrier(jnp.max(logits_teacher, axis=1))
    exp_student = jnp.exp(logits_student - top_student[:, None])
    exp_teacher = jnp.exp(logits_teacher - top_teacher[:, None])
    total_student = lax.optimization_barrier(jnp.sum(exp_student, axis=1))
    total_teacher = lax.optimization_barrier(jnp.sum(exp_teacher, axis=1))
    cross = lax.optimization_barrier(jnp.sum(exp_teacher * logits_student, axis=1))
    loss_rows = -(cross / total_teacher - top_student - jnp.log(total_student))
    differ = exp_student / total_student[:, None] - exp_teacher / total_teacher[:, None]
    logit_gradient = (LOSS_SCALE * weight.astype(jnp.float32)[:, None] * differ / STUDENT_TEMP).astype(jnp.bfloat16)
    return (loss_rows, logit_gradient)

def reference(student_patch_tokens, teacher_patch_tokens, mask_counts, mask_index, student_bottleneck, teacher_bottleneck, student_protos, teacher_protos, center):
    picked = jnp.broadcast_to(mask_index[:, :, None], (IMAGES, MASK_MAX, D))
    student_token_rows = jnp.take_along_axis(student_patch_tokens, picked, axis=1).reshape(IMAGES * MASK_MAX, D)
    teacher_rows = jnp.take_along_axis(teacher_patch_tokens, picked, axis=1).reshape(IMAGES * MASK_MAX, D)
    hidden_student = jnp.dot(student_token_rows, student_bottleneck, preferred_element_type=jnp.float32)
    hidden_teacher = jnp.dot(teacher_rows, teacher_bottleneck, preferred_element_type=jnp.float32)
    inv_student = lax.rsqrt(lax.optimization_barrier(jnp.sum(hidden_student * hidden_student, axis=1, keepdims=True)) + EPSILON)
    inv_teacher = lax.rsqrt(lax.optimization_barrier(jnp.sum(hidden_teacher * hidden_teacher, axis=1, keepdims=True)) + EPSILON)
    units_student = (hidden_student * inv_student).astype(jnp.bfloat16)
    units_teacher = (hidden_teacher * inv_teacher).astype(jnp.bfloat16)
    position = lax.broadcasted_iota(jnp.int32, (IMAGES, MASK_MAX), 1)
    live = position < mask_counts[:, None]
    weight = jnp.where(live, 1.0 / mask_counts.astype(jnp.float32)[:, None], 0.0).astype(jnp.bfloat16)

    def block(proto_acc, items):
        unit_s, unit_t, weight_b = items
        loss_rows, logit_gradient = scores(unit_s, unit_t, weight_b, student_protos, teacher_protos, center)
        image_total = jnp.sum(weight_b.astype(jnp.float32) * loss_rows)
        proto_acc = proto_acc + jnp.dot(unit_s.T, logit_gradient, preferred_element_type=jnp.float32)
        grad_rows = jnp.dot(logit_gradient, student_protos.T, preferred_element_type=jnp.float32)
        return (proto_acc, (image_total, grad_rows))
    init = jnp.zeros((BOT, PROTOS), jnp.float32)
    items = (units_student.reshape(IMAGES, MASK_MAX, BOT), units_teacher.reshape(IMAGES, MASK_MAX, BOT), weight)
    grad_protos, (image_loss, grad_rows) = lax.scan(block, init, items)
    grad_rows = grad_rows.reshape(IMAGES * MASK_MAX, BOT)
    inner = lax.optimization_barrier(jnp.sum(hidden_student * grad_rows, axis=1, keepdims=True))
    grad_hidden = (grad_rows * inv_student - hidden_student * inner * (inv_student * inv_student * inv_student)).astype(jnp.bfloat16)
    grad_bottleneck = jnp.dot(student_token_rows.T, grad_hidden, preferred_element_type=jnp.float32)
    return (image_loss, grad_protos, grad_bottleneck)
```

```python
import functools
import math

import jax
import jax.numpy as jnp
from jax import lax
from jax.experimental import pallas as pl
from jax.experimental.pallas import tpu as pltpu
from jax.sharding import PartitionSpec as P

EPSILON = 1e-06
STUDENT_TEMP = 0.1
TEACHER_TEMP = 0.04
LOSS_SCALE = 4096.0
LOG2E = math.log2(math.e)
SCALE_S = LOG2E / STUDENT_TEMP
SCALE_T = LOG2E / TEACHER_TEMP
LN2 = math.log(2.0)
LANES = 128
F32 = jnp.float32
BF16 = jnp.bfloat16
NT = (((1,), (1,)), ((), ()))
TN = (((0,), (0,)), ((), ()))


def swap(x, axis, size, mask):
    return lax.ppermute(x, axis, [(i, i ^ mask) for i in range(size)])


def core_of(axis="proto"):
    return lax.rem(lax.axis_index(axis), 2)


def whole(shape):
    return pl.BlockSpec(shape, lambda *_: (0,) * len(shape))


def pieces(x):
    hi = x.astype(BF16).astype(F32)
    mid = (x - hi).astype(BF16).astype(F32)
    return hi, mid, x - hi - mid


def project_kernel(st_ref, tt_ref, index_ref, sw_ref, tw_ref, rows_ref, keep_ref, send_ref):
    patches = st_ref.shape[1]
    slots = index_ref.shape[1]
    patch = lax.broadcasted_iota(jnp.int32, (patches, slots), 0)
    picker = (patch == index_ref[...]).astype(F32).T.astype(BF16)
    rows = jnp.dot(picker, st_ref[0], preferred_element_type=F32).astype(BF16)
    rows_ref[...] = rows
    student = jnp.dot(rows, sw_ref[...], preferred_element_type=F32)
    other = jnp.dot(picker, tt_ref[0], preferred_element_type=F32).astype(BF16)
    teacher = jnp.dot(other, tw_ref[...], preferred_element_type=F32)
    first = core_of() == 0

    @pl.when(first)
    def _():
        keep_ref[...] = student
        send_ref[...] = teacher

    @pl.when(jnp.logical_not(first))
    def _():
        keep_ref[...] = teacher
        send_ref[...] = student


def project(st, tt, index, sw, tw):
    slots, width, bot = index.shape[1], st.shape[2], sw.shape[1]
    hid = jax.ShapeDtypeStruct((slots, bot), F32)
    return pl.pallas_call(
        project_kernel,
        out_shape=(jax.ShapeDtypeStruct((slots, width), BF16), hid, hid),
        name="project",
    )(st, tt, index, sw, tw)


def unit_rows(hidden):
    inv = lax.rsqrt(jnp.sum(hidden * hidden, axis=1, keepdims=True) + EPSILON)
    return (hidden * inv).astype(BF16)


def lane_sum(x):
    total = x[:, :LANES]
    for at in range(LANES, x.shape[1], LANES):
        total = total + x[:, at : at + LANES]
    return total


def own_kernel(mine_ref, other_ref, ps_ref, pt_ref, c_ref, units_ref, keep_ref, send_ref,
               ms_ref, mt_ref, ss_ref, st_ref, x_ref, acc_ref):
    step = pl.program_id(0)
    rows, bot = mine_ref.shape
    core = core_of()

    @pl.when(step == 0)
    def _():
        first = core == 0
        mine = unit_rows(mine_ref[...])
        other = unit_rows(other_ref[...])

        @pl.when(first)
        def _():
            units_ref[:, :bot] = mine
            units_ref[:, bot:] = other

        @pl.when(jnp.logical_not(first))
        def _():
            units_ref[:, :bot] = other
            units_ref[:, bot:] = mine

        ms_ref[...] = jnp.full_like(ms_ref, -1e30)
        mt_ref[...] = jnp.full_like(mt_ref, -1e30)
        for ref in (ss_ref, st_ref, x_ref, acc_ref):
            ref[...] = jnp.zeros_like(ref)

    ps = ps_ref[...]
    log_s = jnp.dot(units_ref[:, :bot], ps, preferred_element_type=F32) * SCALE_S
    log_t = (jnp.dot(units_ref[:, bot:], pt_ref[...], preferred_element_type=F32) - c_ref[...]) * SCALE_T
    old_s, old_t = ms_ref[...], mt_ref[...]
    top_s = jnp.maximum(old_s, jnp.max(log_s, axis=1, keepdims=True))
    top_t = jnp.maximum(old_t, jnp.max(log_t, axis=1, keepdims=True))
    ms_ref[...] = top_s
    mt_ref[...] = top_t
    fade_s = jnp.exp2(old_s - top_s)
    fade_t = jnp.exp2(old_t - top_t)
    exp_s = jnp.exp2(log_s - top_s)
    exp_t = jnp.exp2(log_t - top_t)
    ss_ref[...] = ss_ref[...] * fade_s + lane_sum(exp_s)
    st_ref[...] = st_ref[...] * fade_t + lane_sum(exp_t)
    x_ref[...] = x_ref[...] * fade_t + lane_sum(exp_t * log_s)
    acc_ref[:, :bot] = acc_ref[:, :bot] * fade_s + lax.dot_general(
        exp_s.astype(BF16), ps, NT, preferred_element_type=F32)
    acc_ref[:, bot:] = acc_ref[:, bot:] * fade_t + lax.dot_general(
        exp_t.astype(BF16), ps, NT, preferred_element_type=F32)

    @pl.when(step == pl.num_programs(0) - 1)
    def _():
        half = rows // 2
        lane = lax.broadcasted_iota(jnp.int32, (rows, LANES), 1)
        stats = jnp.zeros((rows, LANES), F32)
        columns = (
            ms_ref[...],
            jnp.sum(ss_ref[...], axis=1, keepdims=True),
            mt_ref[...],
            jnp.sum(st_ref[...], axis=1, keepdims=True),
            jnp.sum(x_ref[...], axis=1, keepdims=True),
        )
        for at, column in enumerate(columns):
            stats = jnp.where(lane == at, column, stats)
        first = core == 0

        def write(top_ref, low_ref):
            top_ref[:, : 2 * bot] = acc_ref[:half]
            top_ref[:, 2 * bot :] = stats[:half]
            low_ref[:, : 2 * bot] = acc_ref[half:]
            low_ref[:, 2 * bot :] = stats[half:]

        @pl.when(first)
        def _():
            write(keep_ref, send_ref)

        @pl.when(jnp.logical_not(first))
        def _():
            write(send_ref, keep_ref)


def own_rows(mine, other, ps, pt, center, tile):
    rows, bot = mine.shape
    local = ps.shape[1]
    half = jax.ShapeDtypeStruct((rows // 2, 2 * bot + LANES), F32)
    column = pltpu.VMEM((rows, 1), F32)
    wide = pltpu.VMEM((rows, LANES), F32)
    return pl.pallas_call(
        own_kernel,
        grid=(local // tile,),
        in_specs=[whole(mine.shape), whole(other.shape)]
        + [pl.BlockSpec((bot, tile), lambda j: (0, j))] * 2
        + [pl.BlockSpec((1, tile), lambda j: (0, j))],
        out_specs=[whole((rows, 2 * bot)), whole(half.shape), whole(half.shape)],
        out_shape=(jax.ShapeDtypeStruct((rows, 2 * bot), BF16), half, half),
        scratch_shapes=[column, column, wide, wide, wide, pltpu.VMEM((rows, 2 * bot), F32)],
        name="own_rows",
    )(mine, other, ps, pt, center)


def combine(parts, bot):
    def col(stats, at):
        return stats[:, at : at + 1]

    def tree(values):
        values = list(values)
        while len(values) > 1:
            values = [values[i] + values[i + 1] for i in range(0, len(values), 2)]
        return values[0]

    tops_s = [col(stats, 0) for _, stats in parts]
    tops_t = [col(stats, 2) for _, stats in parts]
    top_s = functools.reduce(jnp.maximum, tops_s)
    top_t = functools.reduce(jnp.maximum, tops_t)
    fade_s = [jnp.exp2(top - top_s) for top in tops_s]
    fade_t = [jnp.exp2(top - top_t) for top in tops_t]
    total_s = tree(col(stats, 1) * fade for (_, stats), fade in zip(parts, fade_s))
    total_t = tree(col(stats, 3) * fade for (_, stats), fade in zip(parts, fade_t))
    cross = tree(col(stats, 4) * fade for (_, stats), fade in zip(parts, fade_t))
    sum_s = tree(sums[:, :bot] * fade for (sums, _), fade in zip(parts, fade_s))
    sum_t = tree(sums[:, bot:] * fade for (sums, _), fade in zip(parts, fade_t))
    return top_s, total_s, top_t, total_t, cross, sum_s, sum_t


def pair_kernel(keep_ref, recv_ref, out_ref):
    bot = (keep_ref.shape[1] - LANES) // 2
    parts = [(ref[:, : 2 * bot], ref[:, 2 * bot :]) for ref in (keep_ref, recv_ref)]
    *stats, sum_s, sum_t = combine(parts, bot)
    out_ref[:, :bot] = sum_s.astype(BF16)
    out_ref[:, bot : 2 * bot] = sum_t.astype(BF16)
    lane = lax.broadcasted_iota(jnp.int32, (keep_ref.shape[0], LANES), 1)
    block = jnp.zeros(lane.shape, F32)
    for at, column in enumerate(stats):
        for piece, part in enumerate(pieces(column)):
            block = jnp.where(lane == at + 8 * piece, part, block)
    out_ref[:, 2 * bot :] = block.astype(BF16)


def pair(keep, recv):
    return pl.pallas_call(
        pair_kernel, out_shape=jax.ShapeDtypeStruct(keep.shape, BF16), name="pair"
    )(keep, recv)


def finish_kernel(shards, counts_ref, mine_ref, other_ref, *refs):
    part_refs, out_ref = refs[:shards], refs[shards]
    bot = mine_ref.shape[1]
    half = out_ref.shape[0]
    core = core_of()
    parts = []
    for ref in part_refs:
        stats = ref[:, 2 * bot :].astype(F32)
        stats = (stats[:, :8] + stats[:, 8:16]) + stats[:, 16:24]
        parts.append((ref[:, : 2 * bot].astype(F32), stats))
    top_s, total_s, top_t, total_t, cross, sum_s, sum_t = combine(parts, bot)
    count = counts_ref[0]
    slot = core * half + lax.broadcasted_iota(jnp.int32, (half, 1), 0)
    divisor = jnp.full((half, 1), count, jnp.int32).astype(F32)
    weight = jnp.where(slot < count, 1.0 / divisor, 0.0).astype(BF16).astype(F32)
    loss = LN2 * (top_s + jnp.log2(total_s) - cross / total_t)
    factor = weight * (LOSS_SCALE / STUDENT_TEMP)
    shift = jnp.where(slot < count, jnp.log2(jnp.maximum(factor, 1e-30)), -1e30)
    out_ref[:, bot:] = jnp.zeros((half, LANES), F32)
    lane = lax.broadcasted_iota(jnp.int32, (half, LANES), 1)
    block = jnp.where(lane == 0, top_s + jnp.log2(total_s) - shift, 0.0)
    block = jnp.where(lane == 1, top_t + jnp.log2(total_t) - shift, block)
    out_ref[:, bot:] = jnp.where(lane == 2, weight * loss, block)
    grad_rows = factor * (sum_s / total_s - sum_t / total_t)
    own = pl.ds(core * half, half)
    hidden = jnp.where(core == 0, mine_ref[own, :], other_ref[own, :])
    inv = lax.rsqrt(jnp.sum(hidden * hidden, axis=1, keepdims=True) + EPSILON)
    inner = jnp.sum(hidden * grad_rows, axis=1, keepdims=True)
    grad_hidden = grad_rows * inv - hidden * inner * (inv * inv * inv)
    out_ref[:, :bot] = grad_hidden


def finish(counts, mine, other, parts):
    half = parts[0].shape[0]
    bot = mine.shape[1]
    specs = [pl.BlockSpec(memory_space=pltpu.SMEM)] + [pl.BlockSpec(memory_space=pltpu.VMEM)] * (2 + len(parts))
    return pl.pallas_call(
        functools.partial(finish_kernel, len(parts)),
        in_specs=specs,
        out_shape=jax.ShapeDtypeStruct((half, bot + LANES), F32),
        name="finish",
    )(counts, mine, other, *parts)


def pack_kernel(images, mine_ref, other_ref, rows_ref, units_ref, loss_ref, block_ref, own_ref, *refs):
    *send_refs, full_ref, both_ref = refs
    half, bot = mine_ref.shape[0], mine_ref.shape[1] - LANES
    slots = 2 * half
    width = rows_ref.shape[1]
    core = core_of()
    first = core == 0

    def place(top_ref, low_ref):
        both_ref[:half] = top_ref[...]
        both_ref[half:] = low_ref[...]

    @pl.when(first)
    def _():
        place(mine_ref, other_ref)

    @pl.when(jnp.logical_not(first))
    def _():
        place(other_ref, mine_ref)

    consts = both_ref[:, bot:]
    loss_ref[0] = jnp.sum(consts[:, 2:3])
    turned = consts.T[:8]
    grad_hidden = both_ref[:, :bot].astype(BF16)
    full_ref[...] = lax.dot_general(grad_hidden, rows_ref[...], TN, preferred_element_type=F32)
    share = bot // images
    at_image = lax.axis_index("img")
    block_ref[...] = full_ref[pl.ds(at_image * share, share), :]
    lines = jnp.concatenate([*pieces(turned)], axis=1).astype(BF16)
    for mask, ref in enumerate([own_ref, *send_refs]):
        ref[:slots] = units_ref[...]
        ref[slots : slots + 8, : 3 * LANES] = lines
        if mask:
            target = lax.bitwise_xor(at_image, mask)
            ref[slots + 16 :, :width] = full_ref[pl.ds(target * share, share), :].astype(BF16)


def pack(mine, other, rows, units, images):
    slots, width = rows.shape
    bot = mine.shape[1] - LANES
    share = bot // images
    send = jax.ShapeDtypeStruct((slots + 16 + share, 2 * bot), BF16)
    specs = [pl.BlockSpec(memory_space=pltpu.SMEM)] + [pl.BlockSpec(memory_space=pltpu.VMEM)] * (1 + images)
    return pl.pallas_call(
        functools.partial(pack_kernel, images),
        out_specs=specs,
        out_shape=[jax.ShapeDtypeStruct((1,), F32), jax.ShapeDtypeStruct((share, width), F32)] + [send] * images,
        scratch_shapes=[pltpu.VMEM((bot, width), F32), pltpu.VMEM((slots, bot + LANES), F32)],
        name="pack",
    )(mine, other, rows, units)


def all_kernel(images, slots, block_ref, *refs):
    pack_refs = refs[:images]
    ps_ref, pt_ref, c_ref, protos_ref, bottleneck_ref, units_ref, turn_ref, consts_ref, grad_ref = refs[images:]
    step = pl.program_id(0)
    share, width = block_ref.shape
    bot = units_ref.shape[1] // 2

    @pl.when(step == 0)
    def _():
        total = block_ref[...]
        for ref in pack_refs[1:]:
            total = total + ref[slots + 16 :, :width].astype(F32)
        bottleneck_ref[...] = total.T
        at_image = lax.axis_index("img")
        for image, ref in enumerate(pack_refs):
            here = slice(image * slots, (image + 1) * slots)
            units_ref[here] = ref[:slots]
            lines = ref[slots : slots + 8, : 3 * LANES].astype(F32)
            lines = (lines[:, :LANES] + lines[:, LANES : 2 * LANES]) + lines[:, 2 * LANES :]
            square = jnp.concatenate([lines, jnp.zeros((LANES - 8, LANES), F32)], axis=0)
            consts_ref[here] = square.T
            turned = ref[:slots, :bot].astype(F32).T
            grad_ref[:bot, :slots] = turned.astype(BF16)
            turn_ref[:, here] = grad_ref[pl.ds(pl.multiple_of(at_image * share, share), share), :slots]

    ps, pt, center = ps_ref[...], pt_ref[...], c_ref[...] * SCALE_T
    for image in range(images):
        here = slice(image * slots, (image + 1) * slots)
        log_s = jnp.dot(units_ref[here, :bot], ps, preferred_element_type=F32) * SCALE_S
        log_t = jnp.dot(units_ref[here, bot:], pt, preferred_element_type=F32) * SCALE_T - center
        grad = jnp.exp2(log_s - consts_ref[here, 0:1]) - jnp.exp2(log_t - consts_ref[here, 1:2])
        grad_ref[here] = grad.astype(BF16)
    protos_ref[...] = jnp.dot(turn_ref[...], grad_ref[...], preferred_element_type=F32)


def all_rows(block, packs, ps, pt, center, tile):
    images = len(packs)
    share, width = block.shape
    bot, local = ps.shape
    slots = packs[0].shape[0] - 16 - share
    rows = images * slots
    return pl.pallas_call(
        functools.partial(all_kernel, images, slots),
        grid=(local // tile,),
        in_specs=[whole(block.shape)]
        + [whole(p.shape) for p in packs]
        + [pl.BlockSpec((bot, tile), lambda j: (0, j))] * 2
        + [pl.BlockSpec((1, tile), lambda j: (0, j))],
        out_specs=[pl.BlockSpec((share, tile), lambda j: (0, j)), whole((width, share))],
        out_shape=(jax.ShapeDtypeStruct((share, local), F32), jax.ShapeDtypeStruct((width, share), F32)),
        scratch_shapes=[
            pltpu.VMEM((rows, 2 * bot), BF16),
            pltpu.VMEM((share, rows), BF16),
            pltpu.VMEM((rows, LANES), F32),
            pltpu.VMEM((max(rows, bot), tile), BF16),
        ],
        name="all_rows",
    )(block, *packs, ps, pt, center)


def per_device(images, shards, st, tt, counts, index, sw, tw, ps, pt, center):
    center = center[None, :]
    zs = range(2, shards, 2)
    rows, keep, send = project(st, tt, index, sw, tw)
    part = keep + swap(send, "proto", shards, 1)

    def tree(values):
        while len(values) > 1:
            values = [values[i] + values[i + 1] for i in range(0, len(values), 2)]
        return values[0]

    mine = tree([part] + [swap(part, "proto", shards, z) for z in zs])
    other = swap(mine, "proto", shards, 1)
    units, keep, send = own_rows(mine, other, ps, pt, center, 1536)
    joined = pair(keep, swap(send, "proto", shards, 1))
    joined = [joined] + [swap(joined, "proto", shards, z) for z in zs]
    done = finish(counts, mine, other, joined)
    loss, block, own, *sends = pack(done, swap(done, "proto", shards, 1), rows, units, images)
    packs = [own] + [swap(s, "img", images, mask + 1) for mask, s in enumerate(sends)]
    grad_protos, grad_bottleneck = all_rows(block, packs, ps, pt, center, 1024)
    return loss, grad_protos, grad_bottleneck


def solution(mesh):
    placed = (
        P("img", None, "proto"),
        P("img", None, "proto"),
        P("img"),
        P("img", None),
        P("proto", None),
        P("proto", None),
        P(None, "proto"),
        P(None, "proto"),
        P("proto"),
    )
    return jax.shard_map(
        functools.partial(per_device, mesh.shape["img"], mesh.shape["proto"]),
        mesh=mesh,
        in_specs=placed,
        out_specs=(P("img"), P("img", "proto"), P("proto", "img")),
        check_vma=False,
    )
```
